32 devices in a mesh: gx: 8 (over z, x), gy: 4 (over y, core).
Axes of the slice: x: 2, y: 2, z: 4, core: 2. Of those that a mesh axis runs over, the one named last changes fastest.
Arguments:
- features: bfloat16 [32, 8192], P(None, ('gx', 'gy')), may hold values from -6 to 6
- offsets: bfloat16 [3, 8192], P(None, ('gx', 'gy')), may hold values from 0 to 16
- point_cell: int32 [8192], P(('gx', 'gy')), may hold values from 0 to 31
- tile_owner: int32 [64, 4], P(('gx', 'gy')), may hold values from 0 to 3, all different within a row; in each aligned block of 2 rows (0 to 1, 2 to 3, ...) at most 2 rows name the same one
- tile_local: int32 [64, 4], P(('gx', 'gy')), may hold values from 0 to 31
- live_count: int32 [64], P(('gx', 'gy')), may hold values from 1 to 4
- w_first: bfloat16 [64, 3], replicated, may hold values from -3.5 to 3.5
- b_first: float32 [64], replicated, may hold values from -3 to 3
- w_second: bfloat16 [64, 64], replicated, may hold values from -0.75 to 0.75
- b_second: float32 [64], replicated, may hold values from -3 to 3
- w_third: bfloat16 [32, 64], replicated, may hold values from -0.75 to 0.75
- w_point: bfloat16 [32, 32], replicated, may hold values from -1 to 1
- b_point: float32 [32], replicated, may hold values from -3 to 3
- w_modes: bfloat16 [32, 32, 32, 2, 32, 32], P(None, 'gx', 'gy'), may hold values from -3 to 3
Outputs:
- latent_out: float32 [32, 32, 32, 128], P('gx', 'gy')
The draws below stay inside these ranges and needn't reach their ends.
Inputs may be any that keep to these rules, and one draw needn't show every extreme that they name: `tile_owner`: each row names 4 different owners; among the rows of one device no owner is named by more than 2 rows.
All inputs are finite; a program needn't handle non-finite values.
Results may differ from the reference program's by a relative error of at most 0.0015.
Values may be sent and summed in bfloat16 or wider, within the bound.
A program may use at most 64 MiB of HBM per device.

```python
import math
import jax
import jax.numpy as jnp
import numpy as np
from jax import lax

C = 32
HID = 64
M = 32
NZ = 128
CX = 4
CY = 8
SPAN = 16
PB = 128
BLK_DEV = 2
LIST = 4
CAP = 2
NX = 32
NY = 32
BLOCKS = 64
POINTS = 8192
COARSE = 32
N_GY = 4
DEVICES = 32


def draw_live_count(key, part):
    key_rows = jax.random.fold_in(key, 11)
    key_slots = jax.random.fold_in(key, 12)
    density = jax.random.randint(key_rows, (DEVICES, 1), 2, LIST + 1)
    lowest = (density + 1) // 2
    raw_draw = jax.random.randint(key_slots, (DEVICES, BLK_DEV), 0, 1 << 20)
    counts = lowest + raw_draw % (density - lowest + 1)
    return counts.reshape(BLOCKS).astype(jnp.int32)


def plant(array, key, smallest, high):
    place = [jax.random.randint(jax.random.fold_in(key, axis), (), 0, length) for axis, length in enumerate(array.shape)]
    widest = array.shape.index(max(array.shape))
    neighbour = place[:widest] + [(place[widest] + 1) % array.shape[widest]] + place[widest + 1:]
    return array.at[tuple(place)].set(smallest).at[tuple(neighbour)].set(high)


def level_of(key, dims, split, least, high):
    factor_of = 1.0
    for dim, shards_of in split:
        draws = jax.random.uniform(jax.random.fold_in(jax.random.fold_in(key, 6), dim), (shards_of,), jnp.float32, least / len(split), high / len(split))
        factor_of = factor_of * jnp.repeat(jnp.exp(draws), dims[dim] // shards_of).reshape((-1,) + (1,) * (len(dims) - 1 - dim))
    return factor_of


def routed_block(key, own, number, rows, amount, top, reach, slope):
    sequence = jax.random.permutation(key, amount)
    heavy_load, ordinary = portions_of(amount, rows * top, reach, slope, True), portions_of(amount, rows * top, reach, slope, False)
    places = jnp.arange(amount)

    def named(tallies, rotation):
        used = int((tallies > 0).sum())
        fixed = max(1, used // 4)
        passed = fixed + (places - fixed + rotation * (used - fixed)) % max(1, amount - fixed)
        return jnp.zeros((amount,), jnp.int32).at[sequence[jnp.where(places < fixed, places, passed)]].set(jnp.asarray(tallies, jnp.int32))

    tallies = jnp.where(number % 4 == 0, named(heavy_load, number // 4), named(ordinary, number - number // 4 - 1))
    mixed = jax.random.permutation(jax.random.fold_in(own, 3), amount)
    giver, taker = mixed[0:amount // 2 * 2:2], mixed[1:amount // 2 * 2:2]
    slack = jnp.minimum(tallies[giver] - 1, reach - tallies[taker]) // 2
    slack = jnp.where((giver == sequence[0]) | (taker == sequence[0]) | (tallies[taker] == 0), 0, jnp.maximum(slack, 0))
    passed = jax.random.randint(jax.random.fold_in(own, 4), (amount // 2,), 0, 1 << 20) % (slack + 1)
    tallies = tallies.at[giver].add(-passed).at[taker].add(passed)
    items = jnp.searchsorted(jnp.cumsum(tallies), jnp.arange(rows * top), side="right").astype(jnp.int32)
    table = items.reshape(top, rows).T
    table = table[jax.random.permutation(jax.random.fold_in(own, 1), rows)]
    rotation = jax.random.randint(jax.random.fold_in(own, 2), (rows, 1), 0, top)
    return jnp.take_along_axis(table, (jnp.arange(top)[None, :] + rotation) % top, axis=1)


def portions_of(count, total, reach, lean, full):
    portions = [(1 << 20) // math.isqrt(standing ** lean) + 1 for standing in range(1, count + 1)]
    largest = reach if full else min(reach, max(-(-total // count), total * portions[0] // sum(portions)))
    least = 1 if total - largest >= count - 1 else 0
    given, spare = [largest] + [least] * (count - 1), total - largest - least * (count - 1)
    while spare > 0:
        movable = [i for i in range(1, count) if given[i] < largest] or [i for i in range(1, count) if given[i] < reach]
        pool, budget = sum([portions[i] for i in movable]), spare
        for i in movable:
            extra = min(reach - given[i], max(1, budget * portions[i] // pool), spare)
            given[i] = given[i] + extra
            spare = spare - extra
    return np.array(given)


def bell_draw(stream_key, shape, spread, limit, pieces=(), kind=jnp.bfloat16):
    result = spread * jax.random.normal(stream_key, shape, jnp.float32)
    if pieces:
        result = result * level_of(stream_key, shape, pieces, -0.22, 0.18)
    return jnp.clip(result, -limit, limit).astype(kind)


def setup_inputs(seed: int = 0) -> dict:
    key_list = jax.random.split(jax.random.key(seed), 15)
    features = bell_draw(key_list[0], (C, POINTS), 1.0, 6.0, ((1, 32),))
    offsets = jnp.clip(16.0 * jax.random.uniform(key_list[1], (3, POINTS), jnp.float32) ** level_of(key_list[1], (3, POINTS), ((1, 32),), -0.2, 0.2), 0.0, 16.0).astype(jnp.bfloat16)
    point_cell = plant(jax.random.randint(key_list[2], (POINTS,), 0, COARSE), jax.random.fold_in(key_list[2], 1), 0, COARSE - 1).astype(jnp.int32)
    tile_owner_keys = jax.random.split(jax.random.fold_in(key_list[3], 1), BLOCKS // BLK_DEV)
    tile_owner_turns = jax.random.permutation(jax.random.fold_in(key_list[3], 3), BLOCKS // BLK_DEV)
    tile_owner = jax.vmap(lambda own, number: routed_block(jax.random.fold_in(key_list[3], 2), own, number, BLK_DEV, N_GY, LIST, CAP, 0))(tile_owner_keys, tile_owner_turns).reshape((BLOCKS, LIST))
    tile_local = plant(jax.random.randint(key_list[4], (BLOCKS, LIST), 0, CX * CY), jax.random.fold_in(key_list[4], 1), 0, (CX * CY) - 1).astype(jnp.int32)
    live_count = draw_live_count(jax.random.fold_in(key_list[14], 71), 0)
    w_first = bell_draw(key_list[6], (HID, 3), 3 ** -0.5, 3.5)
    b_first = bell_draw(key_list[7], (HID,), 0.5, 3.0, (), jnp.float32)
    w_second = bell_draw(key_list[8], (HID, HID), HID ** -0.5, 0.75)
    b_second = bell_draw(key_list[9], (HID,), 0.5, 3.0, (), jnp.float32)
    w_third = bell_draw(key_list[10], (C, HID), HID ** -0.5, 0.75)
    w_point = bell_draw(key_list[11], (C, C), C ** -0.5, 1.0)
    b_point = bell_draw(key_list[12], (C,), 0.5, 3.0, (), jnp.float32)
    w_modes = bell_draw(key_list[13], (M, M, M, 2, C, C), 0.5, 3.0, ((1, 8), (2, 4)))
    return {"features": features, "offsets": offsets, "point_cell": point_cell, "tile_owner": tile_owner, "tile_local": tile_local, "live_count": live_count, "w_first": w_first, "b_first": b_first, "w_second": w_second, "b_second": b_second, "w_third": w_third, "w_point": w_point, "b_point": b_point, "w_modes": w_modes}


def phase_tables(length, modes, two_sided):
    orders = jnp.arange(modes, dtype=jnp.int32)
    if two_sided:
        frequency = jnp.where(orders < modes // 2, orders, length - modes + orders)
    else:
        frequency = orders
    places = jnp.arange(length, dtype=jnp.int32)
    turns = places[:, None] * frequency[None, :] % length
    angles = turns.astype(jnp.float32) * (2.0 * math.pi / length)
    return (jnp.cos(angles), jnp.sin(angles))

def complex_table(length, modes, direction):
    cosine, sine = phase_tables(length, modes, True)
    return jnp.stack([jnp.stack([cosine, direction * sine], -1), jnp.stack([-direction * sine, cosine], -1)], 1)

def inverse_table(length, modes):
    return jnp.transpose(complex_table(length, modes, 1.0), (2, 1, 0, 3))

def real_tables(length, modes, scale):
    cosine, sine = phase_tables(length, modes, False)
    forward = jnp.stack([cosine, -sine], -1) * scale
    inverse = jnp.stack([cosine.T, -sine.T], 1) * scale
    return (forward, inverse)

def pair_sum(block_feats, block_offsets, cell_ids, cell_x, cell_y, weights, grid_dims):
    w_first, b_first, w_second, b_second, w_third = weights
    coarse_y, coarse_z, depth = grid_dims
    along_x = cell_ids // (coarse_y * coarse_z)
    along_y = cell_ids // coarse_z % coarse_y
    along_z = cell_ids % coarse_z
    places = jnp.stack([along_x, along_y, along_z]).astype(jnp.float32) * SPAN + block_offsets.astype(jnp.float32)
    column = jnp.arange(depth, dtype=jnp.int32).astype(jnp.float32)
    centres = jnp.stack([jnp.zeros_like(column) + cell_x.astype(jnp.float32), jnp.zeros_like(column) + cell_y.astype(jnp.float32), column])
    layer_one = w_first.astype(jnp.float32)
    cell_side = layer_one[:, 0:1] * centres[0:1] + layer_one[:, 1:2] * centres[1:2] + layer_one[:, 2:3] * centres[2:3]
    point_side = layer_one[:, 0:1] * places[0:1] + layer_one[:, 1:2] * places[1:2] + layer_one[:, 2:3] * places[2:3]
    inputs = cell_side[:, :, None] - point_side[:, None, :] + b_first[:, None, None]
    hidden = jnp.sin(inputs).astype(jnp.bfloat16).reshape(w_first.shape[0], -1)
    second = jnp.dot(w_second, hidden, preferred_element_type=jnp.float32) + b_second[:, None]
    second = jax.nn.gelu(second).astype(jnp.bfloat16)
    kernel = jnp.dot(w_third, second, preferred_element_type=jnp.float32).reshape(w_third.shape[0], depth, -1)
    return lax.optimization_barrier(jnp.sum(kernel * block_feats.astype(jnp.float32)[:, None, :], axis=2)) / math.sqrt(block_feats.shape[1])

def mix_modes(spectrum, w_modes):
    weights = w_modes.astype(jnp.float32)
    real_in = spectrum[..., 0, :]
    imag_in = spectrum[..., 1, :]
    real_w = weights[..., 0, :, :]
    imag_w = weights[..., 1, :, :]
    form = 'kpqi,kpqio->kpqo'
    best = lax.Precision.HIGHEST
    real_out = jnp.einsum(form, real_in, real_w, precision=best) - jnp.einsum(form, imag_in, imag_w, precision=best)
    imag_out = jnp.einsum(form, real_in, imag_w, precision=best) + jnp.einsum(form, imag_in, real_w, precision=best)
    return jnp.stack([real_out, imag_out], 3)

def fourier_layer(latent, w_point, b_point, w_modes):
    size_x, size_y, channels, depth = latent.shape
    modes = w_modes.shape[0]
    best = lax.Precision.HIGHEST
    scale = 1.0 / math.sqrt(size_x * size_y * depth)
    forward_z, inverse_z = real_tables(depth, modes, scale)
    along_z = jnp.einsum('xycz,zks->xyksc', latent, forward_z, precision=best)
    along_y = jnp.einsum('xyqrc,yrks->xkqsc', along_z, complex_table(size_y, modes, -1.0), precision=best)
    spectrum = jnp.einsum('xpqrc,xrks->kpqsc', along_y, complex_table(size_x, modes, -1.0), precision=best)
    mixed = mix_modes(spectrum, w_modes)
    back_x = jnp.einsum('kpqrc,krxs->xpqsc', mixed, inverse_table(size_x, modes), precision=best)
    back_y = jnp.einsum('xpqrc,prys->xyqsc', back_x, inverse_table(size_y, modes), precision=best)
    spectral = jnp.einsum('xyqrc,qrz->xycz', back_y, inverse_z, precision=best)
    pointwise = jnp.einsum('xycz,co->xyoz', latent, w_point.astype(jnp.float32), precision=best)
    return jax.nn.gelu(spectral + pointwise + b_point[:, None])

def reference(features, offsets, point_cell, tile_owner, tile_local, live_count, w_first, b_first, w_second, b_second, w_third, w_point, b_point, w_modes):
    weights = (w_first, b_first, w_second, b_second, w_third)
    grid_dims = (NY // SPAN, NZ // SPAN, NZ)
    block_feats = features.reshape(C, BLOCKS, PB).transpose(1, 0, 2)
    block_offsets = offsets.reshape(3, BLOCKS, PB).transpose(1, 0, 2)
    block_cells = point_cell.reshape(BLOCKS, PB)
    pair_ids = jnp.arange(BLOCKS * LIST, dtype=jnp.int32)
    block_ids = pair_ids // LIST
    slot_ids = pair_ids % LIST
    row_ids = block_ids // (BLK_DEV * N_GY)
    owners = tile_owner.reshape(-1)
    tile_slot = tile_local.reshape(-1)
    cell_x = CX * row_ids + tile_slot // CY
    cell_y = CY * owners + tile_slot % CY
    is_live = slot_ids < live_count[block_ids]

    def one_pair(pair_index):
        block_now = block_ids[pair_index]
        return lax.cond(is_live[pair_index], lambda: pair_sum(block_feats[block_now], block_offsets[block_now], block_cells[block_now], cell_x[pair_index], cell_y[pair_index], weights, grid_dims), lambda: jnp.zeros((C, NZ), jnp.float32))
    contribs = lax.map(one_pair, pair_ids)
    grid = jnp.zeros((NX * NY, C, NZ), jnp.float32).at[cell_x * NY + cell_y].add(contribs)
    latent = grid.reshape(NX, NY, C, NZ)
    return fourier_layer(latent, w_point, b_point, w_modes)
```

```python
import math

import jax
import jax.numpy as jnp
from jax import lax
from jax.experimental import pallas as pl
from jax.experimental.pallas import tpu as pltpu
from jax.sharding import PartitionSpec as P

NZ = 128
CX = 4
CY = 8
SPAN = 16
PB = 128


def phase_tables(length, modes, two_sided):
    orders = jnp.arange(modes, dtype=jnp.int32)
    if two_sided:
        frequency = jnp.where(orders < modes // 2, orders, length - modes + orders)
    else:
        frequency = orders
    places = jnp.arange(length, dtype=jnp.int32)
    turns = places[:, None] * frequency[None, :] % length
    angles = turns.astype(jnp.float32) * (2.0 * math.pi / length)
    return (jnp.cos(angles), jnp.sin(angles))


def complex_table(length, modes, direction):
    cosine, sine = phase_tables(length, modes, True)
    return jnp.stack(
        [jnp.stack([cosine, direction * sine], -1), jnp.stack([-direction * sine, cosine], -1)], 1
    )


def inverse_table(length, modes):
    return jnp.transpose(complex_table(length, modes, 1.0), (2, 1, 0, 3))


def real_tables(length, modes, scale):
    cosine, sine = phase_tables(length, modes, False)
    forward = jnp.stack([cosine, -sine], -1) * scale
    inverse = jnp.stack([cosine.T, -sine.T], 1) * scale
    return (forward, inverse)


GROUP = 4
ROWS = 8


def pair_kernel(
    owner_ref,
    local_ref,
    live_ref,
    places_ref,
    feats_ref,
    first_ref,
    second_ref,
    third_ref,
    sent_ref,
    cos_p,
    sin_p,
    cos_z,
    sin_z,
):
    blocks, listed = owner_ref.shape
    row_index = lax.axis_index("gx")
    width = second_ref.shape[0]
    hid = width // GROUP
    groups = NZ // GROUP
    scale = 1.0 / math.sqrt(PB)
    linear = 2.0 * math.sqrt(2.0 / math.pi)
    cubic = 4.0 * 0.044715 * linear
    sent_ref[...] = jnp.zeros_like(sent_ref)
    half = 2 * hid
    for block in range(blocks):
        spots = places_ref[pl.ds(block * PB, PB), :]
        point_side = (
            first_ref[0:1, :half] * spots[:, 0:1]
            + first_ref[1:2, :half] * spots[:, 1:2]
            + first_ref[2:3, :half] * spots[:, 2:3]
        )
        cosine, sine = jnp.cos(point_side), jnp.sin(point_side)
        for copy in range(width // half):
            cos_p[block, :, copy * half : (copy + 1) * half] = cosine
            sin_p[block, :, copy * half : (copy + 1) * half] = sine
    lane = lax.broadcasted_iota(jnp.int32, (groups, width), 1)
    group = lax.broadcasted_iota(jnp.int32, (groups, width), 0)
    depth = (group * GROUP + lane // hid).astype(jnp.float32)

    @pl.loop(0, blocks * listed)
    def _(slot):
        block = slot // listed
        place = slot % listed

        @pl.when(place < live_ref[block])
        def _():
            owner = owner_ref[block, place]
            tile = local_ref[block, place]
            cell_x = (CX * row_index + tile // CY).astype(jnp.float32)
            cell_y = (CY * owner + tile % CY).astype(jnp.float32)
            cell_side = (
                first_ref[0:1, :] * cell_x
                + first_ref[1:2, :] * cell_y
                + first_ref[2:3, :] * depth
                + first_ref[3:4, :]
            )
            cos_z[...] = jnp.cos(cell_side)
            sin_z[...] = jnp.sin(cell_side)

            @pl.loop(0, groups // ROWS)
            def _(step):
                start = pl.multiple_of(step * ROWS, ROWS)
                sines = sin_z[pl.ds(start, ROWS), :]
                cosines = cos_z[pl.ds(start, ROWS), :]
                rows = []
                for part in range(ROWS):
                    hidden = (
                        sines[part : part + 1] * cos_p[block]
                        - cosines[part : part + 1] * sin_p[block]
                    ).astype(jnp.bfloat16)
                    half_in = (
                        jnp.dot(hidden, second_ref[...], preferred_element_type=jnp.float32)
                        + first_ref[4:5, :]
                    )
                    bent = jnp.tanh(half_in * (linear + cubic * (half_in * half_in)))
                    second = (half_in + half_in * bent).astype(jnp.bfloat16)
                    kernel = jnp.dot(second, third_ref[...], preferred_element_type=jnp.float32)
                    weighed = kernel * feats_ref[pl.ds(block * PB, PB), :]
                    rows.append(jnp.sum(weighed, axis=0, keepdims=True) * scale)
                sent_ref[owner, block, pl.ds(start, ROWS), :] = jnp.concatenate(rows, axis=0)


def pair_sums(features, offsets, point_cell, tiles, weights, cols_gy, grid_dims):
    w_first, b_first, w_second, b_second, w_third = weights
    tile_owner, tile_local, live_count = tiles
    coarse_y, coarse_z = grid_dims
    channels, hid = w_third.shape
    blocks = live_count.shape[0]
    coarse = jnp.stack(
        [
            point_cell // (coarse_y * coarse_z),
            point_cell // coarse_z % coarse_y,
            point_cell % coarse_z,
        ],
        1,
    )
    places = coarse.astype(jnp.float32) * SPAN + offsets.T.astype(jnp.float32)
    feats = jnp.tile(features.T.astype(jnp.float32), (1, GROUP))
    first = jnp.concatenate(
        [w_first.T.astype(jnp.float32), b_first[None], 0.5 * b_second[None]], 0
    )
    first = jnp.tile(first, (1, GROUP))
    eye = jnp.eye(GROUP, dtype=jnp.bfloat16)
    second = jnp.kron(eye, w_second.T * jnp.bfloat16(0.5))
    third = jnp.kron(eye, w_third.T)
    smem = pl.BlockSpec(memory_space=pltpu.SMEM)
    vmem = pl.BlockSpec(memory_space=pltpu.VMEM)
    width = GROUP * hid
    return pl.pallas_call(
        pair_kernel,
        out_shape=jax.ShapeDtypeStruct(
            (cols_gy, blocks, NZ // GROUP, GROUP * channels), jnp.float32
        ),
        in_specs=[smem] * 3 + [vmem] * 5,
        out_specs=vmem,
        scratch_shapes=[
            pltpu.VMEM((blocks, PB, width), jnp.float32),
            pltpu.VMEM((blocks, PB, width), jnp.float32),
            pltpu.VMEM((NZ // GROUP, width), jnp.float32),
            pltpu.VMEM((NZ // GROUP, width), jnp.float32),
        ],
        name="pair_sums",
    )(tile_owner, tile_local, live_count, places, feats, first, second, third)


def mix_modes(spectrum, w_modes):
    weights = w_modes.astype(jnp.float32)
    real_in = spectrum[..., 0, :]
    imag_in = spectrum[..., 1, :]
    real_w = weights[..., 0, :, :]
    imag_w = weights[..., 1, :, :]
    form = "kpqi,kpqio->kpqo"
    best = lax.Precision.HIGHEST
    real_out = jnp.einsum(form, real_in, real_w, precision=best) - jnp.einsum(
        form, imag_in, imag_w, precision=best
    )
    imag_out = jnp.einsum(form, real_in, imag_w, precision=best) + jnp.einsum(
        form, imag_in, real_w, precision=best
    )
    return jnp.stack([real_out, imag_out], 3)


def local(
    features,
    offsets,
    point_cell,
    tile_owner,
    tile_local,
    live_count,
    w_first,
    b_first,
    w_second,
    b_second,
    w_third,
    w_point,
    b_point,
    w_modes,
):
    best = lax.Precision.HIGHEST
    rows_gx = lax.axis_size("gx")
    cols_gy = lax.axis_size("gy")
    listed = tile_owner.shape[1]
    channels = w_third.shape[0]
    size_x = CX * rows_gx
    size_y = CY * cols_gy
    grid_dims = (size_y // SPAN, NZ // SPAN)
    weights = (w_first, b_first, w_second, b_second, w_third)
    slot_live = jnp.arange(listed, dtype=jnp.int32)[None, :] < live_count[:, None]
    owner_hits = (
        tile_owner[None, :, :] == jnp.arange(cols_gy, dtype=jnp.int32)[:, None, None]
    ) & slot_live[None]
    sent_tiles = jnp.sum(jnp.where(owner_hits, tile_local[None] + 1, 0), axis=2) - 1
    sums = pair_sums(
        features,
        offsets,
        point_cell,
        (tile_owner, tile_local, live_count),
        weights,
        cols_gy,
        grid_dims,
    )
    received = lax.all_to_all(sums, "gy", split_axis=0, concat_axis=0, tiled=True)
    tiles_in = lax.all_to_all(sent_tiles, "gy", split_axis=0, concat_axis=0, tiled=True)
    received = received.reshape(-1, NZ, channels).transpose(0, 2, 1)
    tile_match = (
        tiles_in.reshape(-1)[None, :] == jnp.arange(CX * CY, dtype=jnp.int32)[:, None]
    ).astype(jnp.float32)
    latent = jnp.dot(tile_match, received.reshape(-1, channels * NZ), precision=best).reshape(
        CX, CY, channels, NZ
    )
    modes = w_modes.shape[0]
    scale = 1.0 / math.sqrt(size_x * size_y * NZ)
    forward_z, inverse_z = real_tables(NZ, modes, scale)
    along_z = jnp.einsum("xycz,zks->xyksc", latent, forward_z, precision=best)
    gathered_y = lax.all_to_all(along_z, "gy", split_axis=2, concat_axis=1, tiled=True)
    along_y = jnp.einsum(
        "xyqrc,yrks->xkqsc", gathered_y, complex_table(size_y, modes, -1.0), precision=best
    )
    gathered_x = lax.all_to_all(along_y, "gx", split_axis=1, concat_axis=0, tiled=True)
    spectrum = jnp.einsum(
        "xpqrc,xrks->kpqsc", gathered_x, complex_table(size_x, modes, -1.0), precision=best
    )
    mixed = mix_modes(spectrum, w_modes)
    back_x = jnp.einsum("kpqrc,krxs->xpqsc", mixed, inverse_table(size_x, modes), precision=best)
    returned_x = lax.all_to_all(back_x, "gx", split_axis=0, concat_axis=1, tiled=True)
    back_y = jnp.einsum(
        "xpqrc,prys->xyqsc", returned_x, inverse_table(size_y, modes), precision=best
    )
    returned_y = lax.all_to_all(back_y, "gy", split_axis=1, concat_axis=2, tiled=True)
    spectral = jnp.einsum("xyqrc,qrz->xycz", returned_y, inverse_z, precision=best)
    pointwise = jnp.einsum("xycz,co->xyoz", latent, w_point.astype(jnp.float32), precision=best)
    return jax.nn.gelu(spectral + pointwise + b_point[:, None])


def solution(mesh):
    placed = (
        P(None, ("gx", "gy")),
        P(None, ("gx", "gy")),
        P(("gx", "gy")),
        P(("gx", "gy"), None),
        P(("gx", "gy"), None),
        P(("gx", "gy")),
        P(),
        P(),
        P(),
        P(),
        P(),
        P(),
        P(),
        P(None, "gx", "gy", None, None, None),
    )
    return jax.shard_map(
        local, mesh=mesh, in_specs=placed, out_specs=P("gx", "gy", None, None), check_vma=False
    )
```

```python
import math

import jax
import numpy as np
import jax.numpy as jnp
from jax import lax
from jax.experimental import pallas as pl
from jax.experimental.pallas import tpu as pltpu
from jax.sharding import PartitionSpec as P

NZ = 128
CX = 4
CY = 8
SPAN = 16
PB = 128


GROUP = 4
ROWS = 8


def pair_kernel(
    owner_ref,
    local_ref,
    live_ref,
    places_ref,
    feats_ref,
    first_ref,
    second_ref,
    third_ref,
    table_ref,
    sent_ref,
    chunk_ref,
    cos_p,
    sin_p,
    cos_z,
    sin_z,
    flat,
):
    blocks, listed = owner_ref.shape
    row_index = lax.axis_index("gx")
    width = second_ref.shape[0]
    hid = width // GROUP
    groups = NZ // GROUP
    scale = 1.0 / math.sqrt(PB)
    linear = 2.0 * math.sqrt(2.0 / math.pi)
    cubic = 4.0 * 0.044715 * linear
    sent_ref[...] = jnp.zeros_like(sent_ref)
    half = 2 * hid
    for block in range(blocks):
        spots = places_ref[pl.ds(block * PB, PB), :]
        point_side = (
            first_ref[0:1, :half] * spots[:, 0:1]
            + first_ref[1:2, :half] * spots[:, 1:2]
            + first_ref[2:3, :half] * spots[:, 2:3]
        )
        cosine, sine = jnp.cos(point_side), jnp.sin(point_side)
        for copy in range(width // half):
            cos_p[block, :, copy * half : (copy + 1) * half] = cosine
            sin_p[block, :, copy * half : (copy + 1) * half] = sine
    lane = lax.broadcasted_iota(jnp.int32, (groups, width), 1)
    group = lax.broadcasted_iota(jnp.int32, (groups, width), 0)
    depth = (group + groups * (lane // hid)).astype(jnp.float32)

    @pl.loop(0, blocks * listed)
    def _(slot):
        block = slot // listed
        place = slot % listed

        @pl.when(place < live_ref[block])
        def _():
            owner = owner_ref[block, place]
            tile = local_ref[block, place]
            cell_x = (CX * row_index + tile // CY).astype(jnp.float32)
            cell_y = (CY * owner + tile % CY).astype(jnp.float32)
            cell_side = (
                first_ref[0:1, :] * cell_x
                + first_ref[1:2, :] * cell_y
                + first_ref[2:3, :] * depth
                + first_ref[3:4, :]
            )
            cos_z[...] = jnp.cos(cell_side)
            sin_z[...] = jnp.sin(cell_side)

            @pl.loop(0, groups // ROWS)
            def _(step):
                start = pl.multiple_of(step * ROWS, ROWS)
                sines = sin_z[pl.ds(start, ROWS), :]
                cosines = cos_z[pl.ds(start, ROWS), :]
                rows = []
                for part in range(ROWS):
                    hidden = (
                        sines[part : part + 1] * cos_p[block]
                        - cosines[part : part + 1] * sin_p[block]
                    ).astype(jnp.bfloat16)
                    half_in = (
                        jnp.dot(hidden, second_ref[...], preferred_element_type=jnp.float32)
                        + first_ref[4:5, :]
                    )
                    bent = jnp.tanh(half_in * (linear + cubic * (half_in * half_in)))
                    second = (half_in + half_in * bent).astype(jnp.bfloat16)
                    kernel = jnp.dot(second, third_ref[...], preferred_element_type=jnp.float32)
                    weighed = kernel * feats_ref[pl.ds(block * PB, PB), :]
                    rows.append(jnp.sum(weighed, axis=0, keepdims=True) * scale)
                sent_ref[owner, block, pl.ds(start, ROWS), :] = jnp.concatenate(rows, axis=0)

    cols, rows_c, wide = chunk_ref.shape
    channels = wide // (cols * blocks)
    for dest in range(cols):
        for block in range(blocks):
            item = dest * blocks + block
            for part in range(GROUP):
                flat[
                    part * groups : (part + 1) * groups, item * channels : (item + 1) * channels
                ] = sent_ref[dest, block, :, part * channels : (part + 1) * channels]
    along_z = jnp.dot(
        table_ref[...],
        flat[...],
        precision=lax.Precision.HIGHEST,
        preferred_element_type=jnp.float32,
    )
    items = lax.broadcasted_iota(jnp.int32, (8, wide), 1) // channels
    codes = jnp.full((8, wide), -1.0, jnp.float32)
    for block in range(blocks):
        for place in range(listed):
            owner = owner_ref[block, place]
            tile = local_ref[block, place]
            code = (owner * CX * CY + tile).astype(jnp.float32)
            code = jnp.where(place < live_ref[block], code, -1.0)
            codes = jnp.where(items == owner * blocks + block, code, codes)
    pair = rows_c - 8
    for dest in range(cols):
        chunk_ref[dest, :pair, :] = along_z[dest * pair : (dest + 1) * pair]
        chunk_ref[dest, pair:, :] = codes


def pair_sums(features, offsets, point_cell, tiles, weights, cols_gy, grid_dims, table):
    w_first, b_first, w_second, b_second, w_third = weights
    tile_owner, tile_local, live_count = tiles
    coarse_y, coarse_z = grid_dims
    channels, hid = w_third.shape
    blocks = live_count.shape[0]
    coarse = jnp.stack(
        [
            point_cell // (coarse_y * coarse_z),
            point_cell // coarse_z % coarse_y,
            point_cell % coarse_z,
        ],
        1,
    )
    places = coarse.astype(jnp.float32) * SPAN + offsets.T.astype(jnp.float32)
    feats = jnp.tile(features.T.astype(jnp.float32), (1, GROUP))
    first = jnp.concatenate(
        [w_first.T.astype(jnp.float32), b_first[None], 0.5 * b_second[None]], 0
    )
    first = jnp.tile(first, (1, GROUP))
    eye = jnp.eye(GROUP, dtype=jnp.bfloat16)
    second = jnp.kron(eye, w_second.T * jnp.bfloat16(0.5))
    third = jnp.kron(eye, w_third.T)
    smem = pl.BlockSpec(memory_space=pltpu.SMEM)
    vmem = pl.BlockSpec(memory_space=pltpu.VMEM)
    width = GROUP * hid
    return pl.pallas_call(
        pair_kernel,
        out_shape=(
            jax.ShapeDtypeStruct((cols_gy, blocks, NZ // GROUP, GROUP * channels), jnp.float32),
            jax.ShapeDtypeStruct(
                (cols_gy, table.shape[0] // cols_gy + 8, cols_gy * blocks * channels), jnp.float32
            ),
        ),
        in_specs=[smem] * 3 + [vmem] * 6,
        out_specs=(vmem, vmem),
        scratch_shapes=[
            pltpu.VMEM((blocks, PB, width), jnp.float32),
            pltpu.VMEM((blocks, PB, width), jnp.float32),
            pltpu.VMEM((NZ // GROUP, width), jnp.float32),
            pltpu.VMEM((NZ // GROUP, width), jnp.float32),
            pltpu.VMEM((NZ, cols_gy * blocks * channels), jnp.float32),
        ],
        name="pair_sums",
    )(tile_owner, tile_local, live_count, places, feats, first, second, third, table)


def tables(cols_x, cols_y, modes):
    size_x, size_y = CX * cols_x, CY * cols_y
    own_p, own_q = modes // cols_x, modes // cols_y
    scale = 1.0 / math.sqrt(size_x * size_y * NZ)

    def frequencies(length):
        order = np.arange(modes)
        return np.where(order < modes // 2, order, length - modes + order)

    def turn(angle):
        cosine, sine = np.cos(angle), np.sin(angle)
        return np.array([[cosine, -sine], [sine, cosine]])

    z_turns = 2 * np.pi * (np.outer(np.arange(modes), np.arange(NZ)) % NZ) / NZ
    z_table = np.stack([np.cos(z_turns), -np.sin(z_turns)], 0) * scale
    z_table = z_table.reshape(2, cols_y, own_q, NZ).transpose(1, 0, 2, 3).reshape(-1, NZ)
    x_turns = 2 * np.pi * (np.outer(frequencies(size_x), np.arange(size_x)) % size_x) / size_x
    forward = turn(-x_turns).reshape(2, 2, modes // 4, 4, cols_x, CX)
    eye = np.eye(own_p)
    forward = np.einsum("srgkdx,pP->pgskdrPx", forward, eye).reshape(modes * 2 * own_p, -1)
    swapped = forward.reshape(-1, 2, 4, forward.shape[1])
    swapped = np.stack([-swapped[:, 1], swapped[:, 0]], 1).reshape(forward.shape)
    backward = turn(x_turns).reshape(2, 2, modes // 4, 4, cols_x, CX)
    backward = np.einsum("srgkdx,pP->dsPxpgrk", backward, eye).reshape(-1, modes * 2 * own_p)
    y_turns = 2 * np.pi * (np.outer(frequencies(size_y), np.arange(size_y)) % size_y) / size_y
    lift = turn(y_turns).reshape(2, 2, cols_x, own_p, cols_y, CY)
    lift = np.einsum("srepdy,xX->dsxyerpX", lift, np.eye(CX))
    lift = lift.reshape(2 * CX * size_y, -1)
    inverse = np.stack([np.cos(z_turns), -np.sin(z_turns)], 0) * scale
    inverse = inverse.reshape(2, cols_y, own_q, NZ)
    joined = np.concatenate([forward, swapped], 0)
    return [np.asarray(t, np.float32) for t in (z_table, joined, backward, lift, inverse)]


def fourier_kernel(
    chunk_ref,
    raw_ref,
    forward_ref,
    backward_ref,
    lift_ref,
    modes_ref,
    coded_ref,
    held_ref,
    back_ref,
    weights,
    pieces,
    places,
    sent_b,
    got_c,
    spectra,
    mixed,
    sent_d,
    got_d,
    sent_e,
    load_sem,
    send_y,
    recv_y,
    send_x,
    recv_x,
):
    best = lax.Precision.HIGHEST
    cols_x, cols_y = lax.axis_size("gx"), lax.axis_size("gy")
    mine_x, mine_y = lax.axis_index("gx"), lax.axis_index("gy")
    load = pltpu.make_async_copy(modes_ref, weights, load_sem)
    load.start()
    barrier = pltpu.get_barrier_semaphore()
    for step in range(1, cols_y):
        pl.semaphore_signal(barrier, inc=1, device_id={"gy": lax.rem(mine_y + step, cols_y)})
    for step in range(1, cols_x):
        pl.semaphore_signal(barrier, inc=1, device_id={"gx": lax.rem(mine_x + step, cols_x)})
    pl.semaphore_wait(barrier, cols_x + cols_y - 2)

    def exchange(axis, source, target, sends, recvs, stage):
        count, mine = (cols_x, mine_x) if axis == "gx" else (cols_y, mine_y)
        moves = []
        for step in range(1, count):
            other = lax.rem(mine + step, count)
            move = pltpu.make_async_remote_copy(
                src_ref=source.at[other],
                dst_ref=target.at[mine],
                send_sem=sends.at[stage, step],
                recv_sem=recvs.at[stage, step],
                device_id={axis: other},
            )
            move.start()
            moves.append(move)
        own = pltpu.make_async_copy(source.at[mine], target.at[mine], sends.at[stage, 0])
        own.start()
        return own, moves

    def arrive(started):
        own, moves = started
        own.wait()
        for move in moves:
            move.wait_recv()

    def depart(started):
        for move in started[1]:
            move.wait_send()

    first = exchange("gy", chunk_ref, coded_ref, send_y, recv_y, 0)
    whole = exchange("gy", raw_ref, held_ref, send_y, recv_y, 1)
    arrive(first)
    rows_c, wide = coded_ref.shape[1], coded_ref.shape[2]
    own_q = (rows_c - 8) // 2
    channels = pieces.shape[1] // own_q
    items = wide // channels
    span = items * cols_y
    for item in range(items):
        lanes = slice(item * channels, (item + 1) * channels)
        places[item * cols_y : (item + 1) * cols_y, :] = coded_ref[:, rows_c - 8, lanes]
        for part in range(2):
            for q in range(own_q):
                row = part * span + item * cols_y
                pieces[row : row + cols_y, q * channels : (q + 1) * channels] = coded_ref[
                    :, part * own_q + q, lanes
                ]
    own_p = sent_b.shape[1] // (2 * CX)
    modes = own_p * cols_x
    size_y = CY * cols_y
    code = places[:, 0:1].astype(jnp.int32)
    owner = code // (CX * CY)
    x_at = (code // CY) % CX
    y_at = owner * CY + code % CY
    shape = (span, modes * 2 * CX)
    lane = lax.broadcasted_iota(jnp.int32, shape, 1)
    p_at = (lane // (2 * CX * own_p)) * own_p + (lane // CX) % own_p
    imag = (lane // (CX * own_p)) % 2
    freq = jnp.where(p_at < modes // 2, p_at, size_y - modes + p_at)
    turns = (freq * y_at).astype(jnp.float32) * (1.0 / size_y)
    angle = (turns - jnp.floor(turns)) * (2.0 * math.pi)
    hit = (lane % CX == x_at) & (code >= 0)
    cosine = jnp.where(hit, jnp.cos(angle), 0.0)
    sine = jnp.where(hit, jnp.sin(angle), 0.0)
    upper = jnp.where(imag == 0, cosine, -sine)
    lower = jnp.where(imag == 0, sine, cosine)
    spread = jnp.concatenate([upper, lower], 0)
    along_y = lax.dot_general(
        spread,
        pieces[...],
        (((0,), (0,)), ((), ())),
        precision=best,
        preferred_element_type=jnp.float32,
    )
    sent_b[...] = along_y.reshape(sent_b.shape)
    second = exchange("gx", sent_b, got_c, send_x, recv_x, 0)
    arrive(second)
    lanes_w = pieces.shape[1]
    spectra[...] = jnp.dot(
        forward_ref[...],
        got_c[...].reshape(-1, lanes_w),
        precision=best,
        preferred_element_type=jnp.float32,
    )
    load.wait()
    half = modes * 2 * own_p
    quad = 8 * channels
    row_of = lax.broadcasted_iota(jnp.int32, (8, quad), 0)
    lane_of = lax.broadcasted_iota(jnp.int32, (8, quad), 1)
    keep = lane_of // (2 * channels) == row_of % 4

    @pl.loop(0, half // 8)
    def _(group):
        p = group // (modes // 4)
        low = (group % (modes // 4)) * 4
        start = pl.multiple_of(group * 8, 8)
        plain = spectra[pl.ds(start, 8), :]
        turned = spectra[pl.ds(pl.multiple_of(half + group * 8, 8), 8), :]
        outs = []
        for q in range(own_q):
            lanes = slice(q * channels, (q + 1) * channels)
            both = jnp.concatenate([plain[:, lanes], turned[:, lanes]], 1)
            both = jnp.where(keep, jnp.concatenate([both] * 4, 1), 0.0)
            high = both.astype(jnp.bfloat16)
            rest = (both - high.astype(jnp.float32)).astype(jnp.bfloat16)
            tile = weights[pl.ds(low, 4), p, q].reshape(quad, channels)
            out = jnp.dot(
                jnp.concatenate([high, rest], 0), tile, preferred_element_type=jnp.float32
            )
            outs.append(out[:8] + out[8:])
        mixed[pl.ds(start, 8), :] = jnp.concatenate(outs, 1)

    along_x = jnp.dot(
        backward_ref[...], mixed[...], precision=best, preferred_element_type=jnp.float32
    )
    sent_d[...] = along_x.reshape(sent_d.shape)
    third = exchange("gx", sent_d, got_d, send_x, recv_x, 1)
    arrive(third)
    along_y = jnp.dot(
        lift_ref[...],
        got_d[...].reshape(-1, lanes_w),
        precision=best,
        preferred_element_type=jnp.float32,
    )
    sent_e[...] = along_y.reshape(sent_e.shape)
    fourth = exchange("gy", sent_e, back_ref, send_y, recv_y, 2)
    arrive(fourth)
    arrive(whole)
    for started in (first, whole, second, third, fourth):
        depart(started)


def fourier(chunk, raw, w_modes, forward, backward, lift):
    cols_x, cols_y = lax.axis_size("gx"), lax.axis_size("gy")
    own_p, own_q = w_modes.shape[1:3]
    modes, channels = w_modes.shape[0], w_modes.shape[-1]
    lanes = own_q * channels
    items = chunk.shape[2] // channels
    vmem = pl.BlockSpec(memory_space=pltpu.VMEM)
    parcel = (cols_x, 2 * own_p * CX, lanes)
    last = (cols_y, 2 * CX * CY, lanes)
    f32 = jnp.float32
    return pl.pallas_call(
        fourier_kernel,
        out_shape=(
            jax.ShapeDtypeStruct(chunk.shape, f32),
            jax.ShapeDtypeStruct(raw.shape, f32),
            jax.ShapeDtypeStruct(last, f32),
        ),
        in_specs=[vmem] * 5 + [pl.BlockSpec(memory_space=pl.ANY)],
        out_specs=(vmem, vmem, vmem),
        scratch_shapes=[
            pltpu.VMEM(w_modes.shape, w_modes.dtype),
            pltpu.VMEM((2 * items * cols_y, lanes), f32),
            pltpu.VMEM((items * cols_y, channels), f32),
            pltpu.VMEM(parcel, f32),
            pltpu.VMEM(parcel, f32),
            pltpu.VMEM((forward.shape[0], lanes), f32),
            pltpu.VMEM((forward.shape[0] // 2, lanes), f32),
            pltpu.VMEM(parcel, f32),
            pltpu.VMEM(parcel, f32),
            pltpu.VMEM(last, f32),
            pltpu.SemaphoreType.DMA,
            pltpu.SemaphoreType.DMA((3, cols_y)),
            pltpu.SemaphoreType.DMA((3, cols_y)),
            pltpu.SemaphoreType.DMA((2, cols_x)),
            pltpu.SemaphoreType.DMA((2, cols_x)),
        ],
        compiler_params=pltpu.CompilerParams(collective_id=0, has_side_effects=True),
        name="fourier",
    )(chunk, raw, forward, backward, lift, w_modes)


def local(
    features,
    offsets,
    point_cell,
    tile_owner,
    tile_local,
    live_count,
    w_first,
    b_first,
    w_second,
    b_second,
    w_third,
    w_point,
    b_point,
    w_modes,
):
    best = lax.Precision.HIGHEST
    rows_gx = lax.axis_size("gx")
    cols_gy = lax.axis_size("gy")
    listed = tile_owner.shape[1]
    channels = w_third.shape[0]
    size_y = CY * cols_gy
    grid_dims = (size_y // SPAN, NZ // SPAN)
    weights = (w_first, b_first, w_second, b_second, w_third)
    modes = w_modes.shape[0]
    z_table, forward, backward, lift, inverse = tables(rows_gx, cols_gy, modes)
    sums, chunk = pair_sums(
        features,
        offsets,
        point_cell,
        (tile_owner, tile_local, live_count),
        weights,
        cols_gy,
        grid_dims,
        z_table,
    )
    coded, held, back = fourier(chunk, sums, w_modes, forward, backward, lift)
    blocks_dev = live_count.shape[0]
    codes = coded[:, -8, ::channels].reshape(cols_gy, cols_gy, blocks_dev)
    me = lax.axis_index("gy")
    codes = lax.dynamic_index_in_dim(codes, me, 1, False).reshape(-1)
    received = held.reshape(-1, NZ // GROUP, GROUP, channels).transpose(0, 3, 2, 1)
    received = received.reshape(-1, channels, NZ)
    own_tiles = jnp.arange(CX * CY, dtype=jnp.int32) + me * (CX * CY)
    tile_match = (codes[None, :] == own_tiles[:, None].astype(jnp.float32)).astype(jnp.float32)
    latent = jnp.dot(tile_match, received.reshape(-1, channels * NZ), precision=best)
    latent = latent.reshape(CX, CY, channels, NZ)
    back = back.reshape(cols_gy, 2, CX, CY, -1, channels)
    spectral = jnp.einsum("vsxyqc,svqz->xycz", back, inverse, precision=best)
    pointwise = jnp.einsum("xycz,co->xyoz", latent, w_point.astype(jnp.float32), precision=best)
    return jax.nn.gelu(spectral + pointwise + b_point[:, None])


def solution(mesh):
    placed = (
        P(None, ("gx", "gy")),
        P(None, ("gx", "gy")),
        P(("gx", "gy")),
        P(("gx", "gy"), None),
        P(("gx", "gy"), None),
        P(("gx", "gy")),
        P(),
        P(),
        P(),
        P(),
        P(),
        P(),
        P(),
        P(None, "gx", "gy", None, None, None),
    )
    return jax.shard_map(
        local, mesh=mesh, in_specs=placed, out_specs=P("gx", "gy", None, None), check_vma=False
    )
```

```python
import math

import jax
import numpy as np
import jax.numpy as jnp
from jax import lax
from jax.experimental import pallas as pl
from jax.experimental.pallas import tpu as pltpu
from jax.sharding import PartitionSpec as P

NZ = 128
CX = 4
CY = 8
SPAN = 16
PB = 128


GROUP = 4
ROWS = 8


def pair_kernel(
    owner_ref,
    local_ref,
    live_ref,
    features_ref,
    offsets_ref,
    cells_ref,
    w_first_ref,
    b_first_ref,
    w_second_ref,
    b_second_ref,
    w_third_ref,
    table_ref,
    sent_ref,
    chunk_ref,
    cos_p,
    sin_p,
    cos_z,
    sin_z,
    flat,
    feats_ref,
    first_ref,
    second_ref,
    third_ref,
):
    blocks, listed = owner_ref.shape
    row_index = lax.axis_index("gx")
    width = second_ref.shape[0]
    hid = width // GROUP
    groups = NZ // GROUP
    scale = 1.0 / math.sqrt(PB)
    linear = 2.0 * math.sqrt(2.0 / math.pi)
    cubic = 4.0 * 0.044715 * linear
    sent_ref[...] = jnp.zeros_like(sent_ref)
    half = 2 * hid
    kinds = w_third_ref.shape[0]
    second_ref[...] = jnp.zeros_like(second_ref)
    third_ref[...] = jnp.zeros_like(third_ref)
    turned_two = (w_second_ref[...].astype(jnp.float32).T * 0.5).astype(jnp.bfloat16)
    turned_three = w_third_ref[...].astype(jnp.float32).T.astype(jnp.bfloat16)
    for part in range(GROUP):
        rows = slice(part * hid, (part + 1) * hid)
        second_ref[rows, rows] = turned_two
        third_ref[rows, part * kinds : (part + 1) * kinds] = turned_three
        first_ref[0:3, rows] = w_first_ref[...].astype(jnp.float32)
        first_ref[3:4, rows] = b_first_ref[...]
        first_ref[4:5, rows] = b_second_ref[...] * 0.5
    coarse_y, coarse_z = CY * lax.axis_size("gy") // SPAN, NZ // SPAN
    cells = cells_ref[...]
    coarse = jnp.concatenate(
        [cells // (coarse_y * coarse_z), cells // coarse_z % coarse_y, cells % coarse_z], 0
    )
    places = coarse.astype(jnp.float32) * SPAN + offsets_ref[...].astype(jnp.float32)
    places = jnp.concatenate([places, jnp.zeros((5, places.shape[1]), jnp.float32)], 0)
    features = features_ref[...].astype(jnp.float32)
    for block in range(blocks):
        here = slice(block * PB, (block + 1) * PB)
        turned = features[:, here].T
        feats_ref[here, :] = jnp.concatenate([turned] * GROUP, 1)
        spots = places[:, here].T
        point_side = (
            first_ref[0:1, :half] * spots[:, 0:1]
            + first_ref[1:2, :half] * spots[:, 1:2]
            + first_ref[2:3, :half] * spots[:, 2:3]
        )
        cosine, sine = jnp.cos(point_side), jnp.sin(point_side)
        for copy in range(width // half):
            cos_p[block, :, copy * half : (copy + 1) * half] = cosine
            sin_p[block, :, copy * half : (copy + 1) * half] = sine
    lane = lax.broadcasted_iota(jnp.int32, (groups, width), 1)
    group = lax.broadcasted_iota(jnp.int32, (groups, width), 0)
    depth = (group + groups * (lane // hid)).astype(jnp.float32)

    @pl.loop(0, blocks * listed)
    def _(slot):
        block = slot // listed
        place = slot % listed

        @pl.when(place < live_ref[block])
        def _():
            owner = owner_ref[block, place]
            tile = local_ref[block, place]
            cell_x = (CX * row_index + tile // CY).astype(jnp.float32)
            cell_y = (CY * owner + tile % CY).astype(jnp.float32)
            cell_side = (
                first_ref[0:1, :] * cell_x
                + first_ref[1:2, :] * cell_y
                + first_ref[2:3, :] * depth
                + first_ref[3:4, :]
            )
            cos_z[...] = jnp.cos(cell_side)
            sin_z[...] = jnp.sin(cell_side)

            @pl.loop(0, groups // ROWS)
            def _(step):
                start = pl.multiple_of(step * ROWS, ROWS)
                sines = sin_z[pl.ds(start, ROWS), :]
                cosines = cos_z[pl.ds(start, ROWS), :]
                rows = []
                for part in range(ROWS):
                    hidden = (
                        sines[part : part + 1] * cos_p[block]
                        - cosines[part : part + 1] * sin_p[block]
                    ).astype(jnp.bfloat16)
                    half_in = (
                        jnp.dot(hidden, second_ref[...], preferred_element_type=jnp.float32)
                        + first_ref[4:5, :]
                    )
                    bent = jnp.tanh(half_in * (linear + cubic * (half_in * half_in)))
                    second = (half_in + half_in * bent).astype(jnp.bfloat16)
                    kernel = jnp.dot(second, third_ref[...], preferred_element_type=jnp.float32)
                    weighed = kernel * feats_ref[pl.ds(block * PB, PB), :]
                    rows.append(jnp.sum(weighed, axis=0, keepdims=True) * scale)
                sent_ref[owner, block, pl.ds(start, ROWS), :] = jnp.concatenate(rows, axis=0)

    cols, rows_c, wide = chunk_ref.shape
    channels = wide // (cols * blocks)
    for dest in range(cols):
        for block in range(blocks):
            item = dest * blocks + block
            for part in range(GROUP):
                flat[
                    part * groups : (part + 1) * groups, item * channels : (item + 1) * channels
                ] = sent_ref[dest, block, :, part * channels : (part + 1) * channels]
    along_z = jnp.dot(
        table_ref[...],
        flat[...],
        precision=lax.Precision.HIGHEST,
        preferred_element_type=jnp.float32,
    )
    items = lax.broadcasted_iota(jnp.int32, (8, wide), 1) // channels
    codes = jnp.full((8, wide), -1.0, jnp.float32)
    for block in range(blocks):
        for place in range(listed):
            owner = owner_ref[block, place]
            tile = local_ref[block, place]
            code = (owner * CX * CY + tile).astype(jnp.float32)
            code = jnp.where(place < live_ref[block], code, -1.0)
            codes = jnp.where(items == owner * blocks + block, code, codes)
    pair = rows_c - 8
    for dest in range(cols):
        chunk_ref[dest, :pair, :] = along_z[dest * pair : (dest + 1) * pair]
        chunk_ref[dest, pair:, :] = codes


def pair_sums(features, offsets, point_cell, tiles, weights, cols_gy, table):
    w_first, b_first, w_second, b_second, w_third = weights
    tile_owner, tile_local, live_count = tiles
    channels, hid = w_third.shape
    blocks = live_count.shape[0]
    smem = pl.BlockSpec(memory_space=pltpu.SMEM)
    vmem = pl.BlockSpec(memory_space=pltpu.VMEM)
    width = GROUP * hid
    return pl.pallas_call(
        pair_kernel,
        out_shape=(
            jax.ShapeDtypeStruct((cols_gy, blocks, NZ // GROUP, GROUP * channels), jnp.float32),
            jax.ShapeDtypeStruct(
                (cols_gy, table.shape[0] // cols_gy + 8, cols_gy * blocks * channels), jnp.float32
            ),
        ),
        in_specs=[smem] * 3 + [vmem] * 9,
        out_specs=(vmem, vmem),
        scratch_shapes=[
            pltpu.VMEM((blocks, PB, width), jnp.float32),
            pltpu.VMEM((blocks, PB, width), jnp.float32),
            pltpu.VMEM((NZ // GROUP, width), jnp.float32),
            pltpu.VMEM((NZ // GROUP, width), jnp.float32),
            pltpu.VMEM((NZ, cols_gy * blocks * channels), jnp.float32),
            pltpu.VMEM((blocks * PB, GROUP * channels), jnp.float32),
            pltpu.VMEM((8, width), jnp.float32),
            pltpu.VMEM((width, width), jnp.bfloat16),
            pltpu.VMEM((width, GROUP * channels), jnp.bfloat16),
        ],
        name="pair_sums",
    )(
        tile_owner,
        tile_local,
        live_count,
        features,
        offsets,
        point_cell[None],
        w_first.T,
        b_first[None],
        w_second,
        b_second[None],
        w_third,
        table,
    )


def tables(cols_x, cols_y, modes):
    size_x, size_y = CX * cols_x, CY * cols_y
    own_p, own_q = modes // cols_x, modes // cols_y
    scale = 1.0 / math.sqrt(size_x * size_y * NZ)

    def frequencies(length):
        order = np.arange(modes)
        return np.where(order < modes // 2, order, length - modes + order)

    def turn(angle):
        cosine, sine = np.cos(angle), np.sin(angle)
        return np.array([[cosine, -sine], [sine, cosine]])

    z_turns = 2 * np.pi * (np.outer(np.arange(modes), np.arange(NZ)) % NZ) / NZ
    z_table = np.stack([np.cos(z_turns), -np.sin(z_turns)], 0) * scale
    z_table = z_table.reshape(2, cols_y, own_q, NZ).transpose(1, 0, 2, 3).reshape(-1, NZ)
    x_turns = 2 * np.pi * (np.outer(frequencies(size_x), np.arange(size_x)) % size_x) / size_x
    forward = turn(-x_turns).reshape(2, 2, modes // 4, 4, cols_x, CX)
    eye = np.eye(own_p)
    forward = np.einsum("srgkdx,pP->pgskdrPx", forward, eye).reshape(modes * 2 * own_p, -1)
    swapped = forward.reshape(-1, 2, 4, forward.shape[1])
    swapped = np.stack([-swapped[:, 1], swapped[:, 0]], 1).reshape(forward.shape)
    backward = turn(x_turns).reshape(2, 2, modes // 4, 4, cols_x, CX)
    backward = np.einsum("srgkdx,pP->dsPxpgrk", backward, eye).reshape(-1, modes * 2 * own_p)
    y_turns = 2 * np.pi * (np.outer(frequencies(size_y), np.arange(size_y)) % size_y) / size_y
    lift = turn(y_turns).reshape(2, 2, cols_x, own_p, cols_y, CY)
    lift = np.einsum("srepdy,xX->dsxyerpX", lift, np.eye(CX))
    lift = lift.reshape(2 * CX * size_y, -1)
    inverse = np.stack([np.cos(z_turns), -np.sin(z_turns)], 0) * scale
    inverse = inverse.reshape(2, cols_y, own_q, NZ)
    joined = np.concatenate([forward, swapped], 0)
    return [np.asarray(t, np.float32) for t in (z_table, joined, backward, lift, inverse)]


def fourier_kernel(
    chunk_ref,
    raw_ref,
    forward_ref,
    backward_ref,
    lift_ref,
    modes_ref,
    coded_ref,
    held_ref,
    back_ref,
    weights,
    pieces,
    places,
    sent_b,
    got_c,
    spectra,
    mixed,
    sent_d,
    got_d,
    sent_e,
    load_sem,
    send_y,
    recv_y,
    send_x,
    recv_x,
):
    best = lax.Precision.HIGHEST
    cols_x, cols_y = lax.axis_size("gx"), lax.axis_size("gy")
    mine_x, mine_y = lax.axis_index("gx"), lax.axis_index("gy")
    load = pltpu.make_async_copy(modes_ref, weights, load_sem)
    load.start()
    barrier = pltpu.get_barrier_semaphore()
    for step in range(1, cols_y):
        pl.semaphore_signal(barrier, inc=1, device_id={"gy": lax.rem(mine_y + step, cols_y)})
    for step in range(1, cols_x):
        pl.semaphore_signal(barrier, inc=1, device_id={"gx": lax.rem(mine_x + step, cols_x)})
    pl.semaphore_wait(barrier, cols_x + cols_y - 2)

    def exchange(axis, source, target, sends, recvs, stage):
        count, mine = (cols_x, mine_x) if axis == "gx" else (cols_y, mine_y)
        moves = []
        for step in range(1, count):
            other = lax.rem(mine + step, count)
            move = pltpu.make_async_remote_copy(
                src_ref=source.at[other],
                dst_ref=target.at[mine],
                send_sem=sends.at[stage, step],
                recv_sem=recvs.at[stage, step],
                device_id={axis: other},
            )
            move.start()
            moves.append(move)
        own = pltpu.make_async_copy(source.at[mine], target.at[mine], sends.at[stage, 0])
        own.start()
        return own, moves

    def arrive(started):
        own, moves = started
        own.wait()
        for move in moves:
            move.wait_recv()

    def depart(started):
        for move in started[1]:
            move.wait_send()

    first = exchange("gy", chunk_ref, coded_ref, send_y, recv_y, 0)
    whole = exchange("gy", raw_ref, held_ref, send_y, recv_y, 1)
    arrive(first)
    rows_c, wide = coded_ref.shape[1], coded_ref.shape[2]
    own_q = (rows_c - 8) // 2
    channels = pieces.shape[1] // own_q
    items = wide // channels
    span = items * cols_y
    for item in range(items):
        lanes = slice(item * channels, (item + 1) * channels)
        places[item * cols_y : (item + 1) * cols_y, :] = coded_ref[:, rows_c - 8, lanes]
        for part in range(2):
            for q in range(own_q):
                row = part * span + item * cols_y
                pieces[row : row + cols_y, q * channels : (q + 1) * channels] = coded_ref[
                    :, part * own_q + q, lanes
                ]
    own_p = sent_b.shape[1] // (2 * CX)
    modes = own_p * cols_x
    size_y = CY * cols_y
    code = places[:, 0:1].astype(jnp.int32)
    owner = code // (CX * CY)
    x_at = (code // CY) % CX
    y_at = owner * CY + code % CY
    shape = (span, modes * 2 * CX)
    lane = lax.broadcasted_iota(jnp.int32, shape, 1)
    p_at = (lane // (2 * CX * own_p)) * own_p + (lane // CX) % own_p
    imag = (lane // (CX * own_p)) % 2
    freq = jnp.where(p_at < modes // 2, p_at, size_y - modes + p_at)
    turns = (freq * y_at).astype(jnp.float32) * (1.0 / size_y)
    angle = (turns - jnp.floor(turns)) * (2.0 * math.pi)
    hit = (lane % CX == x_at) & (code >= 0)
    cosine = jnp.where(hit, jnp.cos(angle), 0.0)
    sine = jnp.where(hit, jnp.sin(angle), 0.0)
    upper = jnp.where(imag == 0, cosine, -sine)
    lower = jnp.where(imag == 0, sine, cosine)
    spread = jnp.concatenate([upper, lower], 0)
    along_y = lax.dot_general(
        spread,
        pieces[...],
        (((0,), (0,)), ((), ())),
        precision=best,
        preferred_element_type=jnp.float32,
    )
    sent_b[...] = along_y.reshape(sent_b.shape)
    second = exchange("gx", sent_b, got_c, send_x, recv_x, 0)
    arrive(second)
    lanes_w = pieces.shape[1]
    spectra[...] = jnp.dot(
        forward_ref[...],
        got_c[...].reshape(-1, lanes_w),
        precision=best,
        preferred_element_type=jnp.float32,
    )
    load.wait()
    half = modes * 2 * own_p
    quad = 8 * channels
    row_of = lax.broadcasted_iota(jnp.int32, (8, quad), 0)
    lane_of = lax.broadcasted_iota(jnp.int32, (8, quad), 1)
    keep = lane_of // (2 * channels) == row_of % 4

    @pl.loop(0, half // 8)
    def _(group):
        p = group // (modes // 4)
        low = (group % (modes // 4)) * 4
        start = pl.multiple_of(group * 8, 8)
        plain = spectra[pl.ds(start, 8), :]
        turned = spectra[pl.ds(pl.multiple_of(half + group * 8, 8), 8), :]
        outs = []
        for q in range(own_q):
            lanes = slice(q * channels, (q + 1) * channels)
            both = jnp.concatenate([plain[:, lanes], turned[:, lanes]], 1)
            both = jnp.where(keep, jnp.concatenate([both] * 4, 1), 0.0)
            high = both.astype(jnp.bfloat16)
            rest = (both - high.astype(jnp.float32)).astype(jnp.bfloat16)
            tile = weights[pl.ds(low, 4), p, q].reshape(quad, channels)
            out = jnp.dot(
                jnp.concatenate([high, rest], 0), tile, preferred_element_type=jnp.float32
            )
            outs.append(out[:8] + out[8:])
        mixed[pl.ds(start, 8), :] = jnp.concatenate(outs, 1)

    along_x = jnp.dot(
        backward_ref[...], mixed[...], precision=best, preferred_element_type=jnp.float32
    )
    sent_d[...] = along_x.reshape(sent_d.shape)
    third = exchange("gx", sent_d, got_d, send_x, recv_x, 1)
    arrive(third)
    along_y = jnp.dot(
        lift_ref[...],
        got_d[...].reshape(-1, lanes_w),
        precision=best,
        preferred_element_type=jnp.float32,
    )
    sent_e[...] = along_y.reshape(sent_e.shape)
    fourth = exchange("gy", sent_e, back_ref, send_y, recv_y, 2)
    arrive(fourth)
    arrive(whole)
    for started in (first, whole, second, third, fourth):
        depart(started)


def fourier(chunk, raw, w_modes, forward, backward, lift):
    cols_x, cols_y = lax.axis_size("gx"), lax.axis_size("gy")
    own_p, own_q = w_modes.shape[1:3]
    modes, channels = w_modes.shape[0], w_modes.shape[-1]
    lanes = own_q * channels
    items = chunk.shape[2] // channels
    vmem = pl.BlockSpec(memory_space=pltpu.VMEM)
    parcel = (cols_x, 2 * own_p * CX, lanes)
    last = (cols_y, 2 * CX * CY, lanes)
    f32 = jnp.float32
    return pl.pallas_call(
        fourier_kernel,
        out_shape=(
            jax.ShapeDtypeStruct(chunk.shape, f32),
            jax.ShapeDtypeStruct(raw.shape, f32),
            jax.ShapeDtypeStruct(last, f32),
        ),
        in_specs=[vmem] * 5 + [pl.BlockSpec(memory_space=pl.ANY)],
        out_specs=(vmem, vmem, vmem),
        scratch_shapes=[
            pltpu.VMEM(w_modes.shape, w_modes.dtype),
            pltpu.VMEM((2 * items * cols_y, lanes), f32),
            pltpu.VMEM((items * cols_y, channels), f32),
            pltpu.VMEM(parcel, f32),
            pltpu.VMEM(parcel, f32),
            pltpu.VMEM((forward.shape[0], lanes), f32),
            pltpu.VMEM((forward.shape[0] // 2, lanes), f32),
            pltpu.VMEM(parcel, f32),
            pltpu.VMEM(parcel, f32),
            pltpu.VMEM(last, f32),
            pltpu.SemaphoreType.DMA,
            pltpu.SemaphoreType.DMA((3, cols_y)),
            pltpu.SemaphoreType.DMA((3, cols_y)),
            pltpu.SemaphoreType.DMA((2, cols_x)),
            pltpu.SemaphoreType.DMA((2, cols_x)),
        ],
        compiler_params=pltpu.CompilerParams(collective_id=0, has_side_effects=True),
        name="fourier",
    )(chunk, raw, forward, backward, lift, w_modes)


def local(
    features,
    offsets,
    point_cell,
    tile_owner,
    tile_local,
    live_count,
    w_first,
    b_first,
    w_second,
    b_second,
    w_third,
    w_point,
    b_point,
    w_modes,
):
    best = lax.Precision.HIGHEST
    rows_gx = lax.axis_size("gx")
    cols_gy = lax.axis_size("gy")
    listed = tile_owner.shape[1]
    channels = w_third.shape[0]
    weights = (w_first, b_first, w_second, b_second, w_third)
    modes = w_modes.shape[0]
    z_table, forward, backward, lift, inverse = tables(rows_gx, cols_gy, modes)
    sums, chunk = pair_sums(
        features,
        offsets,
        point_cell,
        (tile_owner, tile_local, live_count),
        weights,
        cols_gy,
        z_table,
    )
    coded, held, back = fourier(chunk, sums, w_modes, forward, backward, lift)
    blocks_dev = live_count.shape[0]
    codes = coded[:, -8, ::channels].reshape(cols_gy, cols_gy, blocks_dev)
    me = lax.axis_index("gy")
    codes = lax.dynamic_index_in_dim(codes, me, 1, False).reshape(-1)
    received = held.reshape(-1, NZ // GROUP, GROUP, channels).transpose(0, 3, 2, 1)
    received = received.reshape(-1, channels, NZ)
    own_tiles = jnp.arange(CX * CY, dtype=jnp.int32) + me * (CX * CY)
    tile_match = (codes[None, :] == own_tiles[:, None].astype(jnp.float32)).astype(jnp.float32)
    latent = jnp.dot(tile_match, received.reshape(-1, channels * NZ), precision=best)
    latent = latent.reshape(CX, CY, channels, NZ)
    back = back.reshape(cols_gy, 2, CX, CY, -1, channels)
    spectral = jnp.einsum("vsxyqc,svqz->xycz", back, inverse, precision=best)
    pointwise = jnp.einsum("xycz,co->xyoz", latent, w_point.astype(jnp.float32), precision=best)
    return jax.nn.gelu(spectral + pointwise + b_point[:, None])


def solution(mesh):
    placed = (
        P(None, ("gx", "gy")),
        P(None, ("gx", "gy")),
        P(("gx", "gy")),
        P(("gx", "gy"), None),
        P(("gx", "gy"), None),
        P(("gx", "gy")),
        P(),
        P(),
        P(),
        P(),
        P(),
        P(),
        P(),
        P(None, "gx", "gy", None, None, None),
    )
    return jax.shard_map(
        local, mesh=mesh, in_specs=placed, out_specs=P("gx", "gy", None, None), check_vma=False
    )
```
